32 devices in a mesh: col: 4 (over y, x), wide: 8 (over z, core).
Axes of the slice: x: 2, y: 2, z: 4, core: 2. Of those that a mesh axis runs over, the one named last changes fastest.
Arguments:
- flux_jac: bfloat16 [768, 320, 320], P(('col', 'wide')), may hold values from -0.3125 to 0.3125
- dissipation: float32 [768], P(('col', 'wide')), may hold values from 0.1 to 0.4
- basis: bfloat16 [512, 320, 128], P(('col', 'wide')), may hold values from -0.5 to 0.5
- residual: bfloat16 [64, 2560], P(('col', 'wide')), may hold values from -6 to 6
- face_elems: int32 [768, 2], P(('col', 'wide')), may hold values from 0 to 7, as said below
- primal: int32 [64, 128], P(('col', 'wide')), may hold values from 0 to 4095, as said below
- coarse_owner: int32 [4096], replicated, may hold values from 0 to 4095, as said below
- counts: int32 [64], P(('col', 'wide')), may hold values from 32 to 128, as said below
Outputs:
- correction: float32 [64, 2560], P(('col', 'wide'))
- coarse_solution: float32 [4096], P(('col', 'wide'))
The draws below stay inside these ranges and needn't reach their ends.
Inputs may be any that keep to these rules, and one draw needn't show every extreme that they name: `face_elems`: local element numbers inside the face's subdomain; the two elements of a face differ. `primal`: the 128 entries of a subdomain are distinct. Among the live entries (position below counts) of the subdomains of one device, at most 64 have coarse_owner slots in one owner column (slot // 1024), and in every draw some devices reach 64 for every owner column. `coarse_owner`: A permutation of the 4096 slots. Slot t belongs to owner column t // 1024, and to the device with index t // 128 along col+wide. `counts`: in every draw all subdomains of some wide index have 128 live constraints.
All inputs are finite; a program needn't handle non-finite values.
Results may differ from the reference program's by a relative error of at most 0.0042.
Values may be sent and summed in bfloat16 or wider, within the bound.
A program may use at most 64 MiB of HBM per device.

```python
import math
import jax
import jax.numpy as jnp
from jax import lax

NU = 320
P_SIZE = 128
ELS = 8
FACE_SUB = 12
ITERS = 3
SUB_DEV = 2
CO_DEV = 128
SUBDOMAINS = 64
NCC = 1024
NC = 4096


def owner_perm(key):
    return jax.random.permutation(jax.random.fold_in(key, 11), NC).astype(jnp.int32)


def draw_coarse_owner(key, part):
    return owner_perm(key)


def draw_primal(key, part):
    table = owner_perm(key)
    inverse = jnp.argsort(table).astype(jnp.int32)
    col_count = NC // NCC
    sub_keys = jax.random.split(jax.random.fold_in(key, 23), SUBDOMAINS)

    def one_subdomain(sub_key):
        row_key, dof_key = jax.random.split(sub_key)
        row_order = jax.random.permutation(row_key, P_SIZE).astype(jnp.int32)
        column = row_order // (P_SIZE // col_count)
        within = jax.random.permutation(dof_key, NCC)[:P_SIZE].astype(jnp.int32)
        return column * NCC + within
    slot_draw = jax.vmap(one_subdomain)(sub_keys)
    return inverse[slot_draw].astype(jnp.int32)


def draw_counts(key, part):
    wide_count = NCC // CO_DEV
    base_key, wide_key = jax.random.split(jax.random.fold_in(key, 31))
    drawn = jax.random.randint(base_key, (SUBDOMAINS,), P_SIZE // 4, P_SIZE // 2 + 1)
    full_wide = jax.random.randint(wide_key, (), 0, wide_count)
    device = jnp.arange(SUBDOMAINS, dtype=jnp.int32) // SUB_DEV
    return jnp.where(device % wide_count == full_wide, P_SIZE, drawn).astype(jnp.int32)


def draw_face_elems(key, part):
    first_key, step_key = jax.random.split(jax.random.fold_in(key, 41))
    face_total = SUBDOMAINS * FACE_SUB
    first_elem = jax.random.randint(first_key, (face_total,), 0, ELS)
    elem_step = jax.random.randint(step_key, (face_total,), 1, ELS)
    return jnp.stack([first_elem, (first_elem + elem_step) % ELS], axis=1).astype(jnp.int32)


def shard_levels(stream_key, extent, pieces, low, largest):
    def one(axis_at, blocks):
        draws = jax.random.uniform(jax.random.fold_in(jax.random.fold_in(stream_key, 6), axis_at), (blocks,), jnp.float32, low / len(pieces), largest / len(pieces))
        return jnp.repeat(jnp.exp(draws), extent[axis_at] // blocks).reshape((-1,) + (1,) * (len(extent) - axis_at - 1))

    factor_of = one(*pieces[0])
    for cut in pieces[1:]:
        factor_of = factor_of * one(*cut)
    return factor_of


def noise(rng, shape, scale, bound, cuts=(), kind=jnp.bfloat16):
    array = jax.random.normal(rng, shape, jnp.float32) * scale
    if len(cuts) > 0:
        array = shard_levels(rng, shape, cuts, -0.22, 0.18) * array
    return jnp.clip(array, min=-bound, max=bound).astype(kind)


def setup_inputs(seed: int = 0) -> dict:
    key_list = jax.random.split(jax.random.key(seed), 9)
    return {
        "flux_jac": noise(key_list[0], (SUBDOMAINS * FACE_SUB, NU, NU), NU ** -0.5, 0.3125, ((0, 32),)),
        "dissipation": jnp.clip(jnp.exp(math.log(0.4) - 1.3862944 * jax.random.uniform(key_list[1], (SUBDOMAINS * FACE_SUB,), jnp.float32) ** shard_levels(key_list[1], (SUBDOMAINS * FACE_SUB,), ((0, 32),), -0.2, 0.2)), 0.1, 0.4),
        "basis": noise(key_list[2], (SUBDOMAINS * ELS, NU, P_SIZE), P_SIZE ** -0.5, 0.5, ((0, 32),)),
        "residual": noise(key_list[3], (SUBDOMAINS, ELS * NU), 1.0, 6.0, ((0, 32),)),
        "face_elems": draw_face_elems(jax.random.fold_in(key_list[8], 71), 0),
        "primal": draw_primal(jax.random.fold_in(key_list[8], 71), 0),
        "coarse_owner": draw_coarse_owner(jax.random.fold_in(key_list[8], 71), 0),
        "counts": draw_counts(jax.random.fold_in(key_list[8], 71), 0),
    }


damping = 0.7


def subdomain_terms(packed):
    face_jac, face_diss, sub_basis, face_pairs, sub_res, alive_mask = packed
    basis_a = sub_basis[face_pairs[:, 0]].astype(jnp.float32)
    basis_b = sub_basis[face_pairs[:, 1]].astype(jnp.float32)
    paired = (basis_a + basis_b).astype(jnp.bfloat16)
    flux_term = jnp.einsum("fij,fjp->fip", face_jac.astype(jnp.float32), paired.astype(jnp.float32), precision=lax.Precision.HIGHEST)
    face_term = 0.5 * flux_term + (0.5 * face_diss)[:, None, None] * (basis_a - basis_b)
    elem_image = jax.ops.segment_sum(face_term, face_pairs[:, 0], num_segments=ELS).astype(jnp.bfloat16)
    flat_basis = sub_basis.reshape(ELS * NU, P_SIZE)
    schur_block = jnp.dot(flat_basis.T, elem_image.reshape(ELS * NU, P_SIZE), preferred_element_type=jnp.float32)
    schur_block = schur_block * alive_mask[:, None] * alive_mask[None, :]
    load_vec = jnp.dot(sub_res, flat_basis, preferred_element_type=jnp.float32) * alive_mask
    return schur_block, load_vec


def correct_one(packed):
    sub_basis, near_sol = packed
    return jnp.dot(sub_basis, near_sol, preferred_element_type=jnp.float32)


def reference(flux_jac, dissipation, basis, residual, face_elems, primal, coarse_owner, counts):
    alive_mask = (jnp.arange(P_SIZE, dtype=jnp.int32)[None, :] < counts[:, None]).astype(jnp.float32)
    packed = (flux_jac.reshape(SUBDOMAINS, FACE_SUB, NU, NU), dissipation.reshape(SUBDOMAINS, FACE_SUB),
              basis.reshape(SUBDOMAINS, ELS, NU, P_SIZE), face_elems.reshape(SUBDOMAINS, FACE_SUB, 2),
              residual, alive_mask)
    schur_block, load_vec = lax.map(subdomain_terms, packed)
    slot_of = coarse_owner[primal].astype(jnp.int32)
    flat_slot = slot_of.reshape(-1)
    coarse_load = jax.ops.segment_sum(load_vec.reshape(-1), flat_slot, num_segments=NC)
    diag_vals = jnp.diagonal(schur_block, axis1=1, axis2=2)
    coarse_diag = jax.ops.segment_sum(diag_vals.reshape(-1), flat_slot, num_segments=NC)
    diag_floor = jnp.maximum(coarse_diag, 1.0)

    def apply_op(field):
        gathered = field[slot_of]
        rows_out = jnp.einsum("spq,sq->sp", schur_block, gathered, precision=lax.Precision.HIGHEST)
        return jax.ops.segment_sum(rows_out.reshape(-1), flat_slot, num_segments=NC)

    solution = damping * coarse_load / diag_floor
    for sweep_idx in range(ITERS):
        solution = solution + damping * (coarse_load - apply_op(solution)) / diag_floor
    near_sol = (solution[slot_of] * alive_mask).astype(jnp.bfloat16)
    correction = lax.map(correct_one, (basis.reshape(SUBDOMAINS, ELS * NU, P_SIZE), near_sol))
    return correction, solution
```

```python
import functools

import jax
import jax.numpy as jnp
from jax import lax
from jax.experimental import pallas as pl
from jax.experimental.pallas import tpu as pltpu
from jax.sharding import PartitionSpec as P

ITERS = 3
damping = 0.7
F32 = jnp.float32
BF16 = jnp.bfloat16
MESH = pl.DeviceIdType.MESH


def split2(value):
    high = value.astype(BF16)
    return high, (value - high.astype(F32)).astype(BF16)


def dot(lhs, rhs):
    return jnp.dot(lhs, rhs, preferred_element_type=F32)


def onehot_dot(onehot, value):
    width = value.shape[1]
    both = dot(onehot, jnp.concatenate(split2(value), axis=1))
    return both[:, :width] + both[:, width:]


def column(row, size):
    return jnp.transpose(jnp.broadcast_to(row, (size, size)))


def pick_row(value, row):
    return jnp.sum(jnp.where(iota(value.shape, 0) == row, value, 0.0), axis=0, keepdims=True)


def iota(shape, axis):
    return lax.broadcasted_iota(jnp.int32, shape, axis)


def local_kernel(
    dims, faces_ref, diss_ref, counts_ref, flux_ref, basis_ref, res_ref, primal_ref, owner_ref,
    schur_ref, load_ref, high_ref, low_ref, image,
):
    step_faces, steps_sub, elem_sub, units, prim = dims
    step = pl.program_id(0)
    sub = step // steps_sub
    part = step % steps_sub

    @pl.when(part == 0)
    def _():
        image[...] = jnp.zeros_like(image)

    for k in range(step_faces):
        face = step * step_faces + k
        first = faces_ref[face, 0]
        second = faces_ref[face, 1]
        basis_a = basis_ref[sub * elem_sub + first].astype(F32)
        basis_b = basis_ref[sub * elem_sub + second].astype(F32)
        flux = dot(flux_ref[k], (basis_a + basis_b).astype(BF16))
        image[first] += 0.5 * flux + (0.5 * diss_ref[face]) * (basis_a - basis_b)

    @pl.when(part == steps_sub - 1)
    def _():
        alive_col = (iota((prim, prim), 0) < counts_ref[sub]).astype(F32)
        alive_row = (iota((prim, prim), 1) < counts_ref[sub]).astype(F32)
        flat = basis_ref[pl.ds(sub * elem_sub, elem_sub)].reshape(elem_sub * units, prim)
        img = image[...].reshape(elem_sub * units, prim).astype(BF16)
        schur = lax.dot_general(flat, img, (((0,), (0,)), ((), ())), preferred_element_type=F32)
        schur_ref[...] = schur * alive_col * alive_row
        residual = pick_row(res_ref[...].astype(F32), sub).astype(BF16)
        load_ref[...] = column(dot(residual, flat), prim) * alive_col
        dof = column(pick_row(primal_ref[...].astype(F32), sub), prim).astype(jnp.int32)
        owner = owner_ref[...]
        rows = owner.shape[0]
        pick = ((dof[:, :1] >> 7) == iota((prim, rows), 1)).astype(F32).astype(BF16)
        table = jnp.concatenate(
            [(owner >> 7).astype(F32).astype(BF16), (owner & 127).astype(F32).astype(BF16)], axis=1
        )
        found = dot(pick, table)
        lane = ((dof & 127) == iota((prim, 128), 1)).astype(F32)
        high = jnp.sum(found[:, :128] * lane, axis=1, keepdims=True)
        low = jnp.sum(found[:, 128:] * lane, axis=1, keepdims=True)
        high_ref[...] = jnp.broadcast_to(high, (prim, 128))
        low_ref[...] = jnp.broadcast_to(low, (prim, 128))


def sweep_kernel(
    dims, counts_ref, schur_ref, load_ref, high_ref, low_ref, basis_ref,
    corr_ref, sol_ref, basis_buf, out0, in0, outs, ins, shares, mine, send_sem, recv_sem, copy_sem,
):
    col_count, wide_count, sub_count, prim = dims
    n = col_count * wide_count
    rows = sub_count * prim
    me = lax.axis_index("col") * wide_count + lax.axis_index("wide")

    def peer(k):
        to = lax.rem(me + k, n)
        return to, (to // wide_count, lax.rem(to, wide_count))

    barrier = pltpu.get_barrier_semaphore()

    @pl.loop(1, n)
    def _(k):
        pl.semaphore_signal(barrier, inc=1, device_id=peer(k)[1], device_id_type=MESH)

    fetch = pltpu.make_async_copy(basis_ref, basis_buf, copy_sem)
    fetch.start()

    schur_high, schur_low = split2(schur_ref[...])
    high = high_ref[...].astype(jnp.int32)
    low_hot = (low_ref[...].astype(jnp.int32) == iota((rows, 128), 1)).astype(F32)
    row_hot = (high[:, :1] == iota((rows, n), 1)).astype(F32).astype(BF16)
    hots = []
    for sub in range(sub_count):
        part = jnp.transpose(high_ref[pl.ds(sub * prim, prim), :])[:1, :].astype(jnp.int32)
        hots.append((jnp.broadcast_to(part, (n, prim)) == iota((n, prim), 0)).astype(F32).astype(BF16))
    row_hot_t = jnp.concatenate(hots, axis=1)

    diag = jnp.concatenate(
        [
            jnp.sum(
                schur_ref[pl.ds(sub * prim, prim), :]
                * (iota((prim, prim), 0) == iota((prim, prim), 1)).astype(F32),
                axis=1, keepdims=True,
            )
            for sub in range(sub_count)
        ],
        axis=0,
    )
    start = onehot_dot(
        row_hot_t, jnp.concatenate([load_ref[...] * low_hot, diag * low_hot], axis=1)
    )
    out0[...] = start.reshape(n, 1, 256)
    pl.semaphore_wait(barrier, n - 1)

    def scatter_out(source, target, hop):
        @pl.loop(1, n)
        def _(k):
            to, where = peer(k)
            pltpu.make_async_remote_copy(
                src_ref=source.at[to], dst_ref=target.at[me],
                send_sem=send_sem.at[hop], recv_sem=recv_sem.at[hop],
                device_id=where, device_id_type=MESH,
            ).start()

        target[me] = source[me]

    def arrived(target, hop):
        some = target.at[pl.ds(0, n - 1)]
        pltpu.make_async_copy(some, some, recv_sem.at[hop]).wait()

    def left(target, hop):
        some = target.at[pl.ds(0, n - 1)]
        pltpu.make_async_copy(some, some, send_sem.at[hop]).wait()

    def share(value, rnd):
        mine[rnd] = value

        @pl.loop(1, n)
        def _(k):
            to, where = peer(k)
            pltpu.make_async_remote_copy(
                src_ref=mine.at[rnd], dst_ref=shares.at[rnd, me],
                send_sem=send_sem.at[2 * rnd + 1], recv_sem=recv_sem.at[2 * rnd + 1],
                device_id=where, device_id_type=MESH,
            ).start()

        shares[rnd, me] = value
        arrived(shares.at[rnd], 2 * rnd + 1)
        whole = shares[rnd].reshape(n, 128)
        return onehot_dot(row_hot, whole) * low_hot

    scatter_out(out0, in0, 0)
    arrived(in0, 0)
    total = jnp.sum(in0[...], axis=0)
    load_own = total[:, :128]
    scale = damping / jnp.maximum(total[:, 128:], 1.0)
    current = load_own * scale
    for rnd in range(ITERS):
        spread = share(current, rnd)
        sp_high, sp_low = split2(spread)
        prods = []
        for sub in range(sub_count):
            part = slice(sub * prim, (sub + 1) * prim)
            both = dot(schur_high[part], jnp.concatenate([sp_high[part], sp_low[part]], axis=1))
            prods.append(both[:, :128] + both[:, 128:] + dot(schur_low[part], sp_high[part]))
        row_value = jnp.sum(jnp.concatenate(prods, axis=0), axis=1, keepdims=True)
        outs[rnd] = onehot_dot(row_hot_t, row_value * low_hot).reshape(n, 1, 128)
        scatter_out(outs.at[rnd], ins.at[rnd], 2 * rnd + 2)
        arrived(ins.at[rnd], 2 * rnd + 2)
        current = current + (load_own - jnp.sum(ins[rnd], axis=0)) * scale
    sol_ref[...] = current
    near = jnp.sum(share(current, ITERS), axis=1, keepdims=True)
    fetch.wait()
    for sub in range(sub_count):
        near_sub = jnp.broadcast_to(near[sub * prim:(sub + 1) * prim], (prim, prim))
        alive = (iota((prim, prim), 0) < counts_ref[sub]).astype(F32)
        near_row = jnp.transpose(near_sub * alive)[:16].astype(BF16)
        found = lax.dot_general(
            near_row, basis_buf[sub], (((1,), (1,)), ((), ())), preferred_element_type=F32
        )
        corr_ref[pl.ds(sub, 1), :] = found[:1]
    left(in0, 0)
    for rnd in range(ITERS + 1):
        left(shares.at[rnd], 2 * rnd + 1)
    for rnd in range(ITERS):
        left(ins.at[rnd], 2 * rnd + 2)


def body(flux_jac, dissipation, basis, residual, face_elems, primal, coarse_owner, counts):
    col_count = lax.axis_size("col")
    wide_count = lax.axis_size("wide")
    n = col_count * wide_count
    sub_count = residual.shape[0]
    face_count = flux_jac.shape[0]
    elem_sub = basis.shape[0] // sub_count
    units, prim = basis.shape[1:]
    rows = sub_count * prim
    step_faces = 4
    steps = face_count // step_faces
    steps_sub = steps // sub_count
    smem = pl.BlockSpec(memory_space=pltpu.SMEM)
    vmem = pl.BlockSpec(memory_space=pltpu.VMEM)
    block = pl.BlockSpec((prim, 128), lambda i: (i // steps_sub, 0))
    schur, load, high, low = pl.pallas_call(
        functools.partial(local_kernel, (step_faces, steps_sub, elem_sub, units, prim)),
        grid=(steps,),
        in_specs=[
            smem, smem, smem,
            pl.BlockSpec((step_faces, units, units), lambda i: (i, 0, 0)),
            vmem, vmem, vmem, vmem,
        ],
        out_specs=[block] * 4,
        out_shape=[jax.ShapeDtypeStruct((rows, 128), F32)] * 4,
        scratch_shapes=[pltpu.VMEM((elem_sub, units, prim), F32)],
        compiler_params=pltpu.CompilerParams(vmem_limit_bytes=32 << 20),
        name="local",
    )(face_elems, dissipation, counts, flux_jac, basis, residual, primal,
      coarse_owner.reshape(-1, 128))
    basis_sub = basis.reshape(sub_count, elem_sub * units, prim)
    correction, own = pl.pallas_call(
        functools.partial(sweep_kernel, (col_count, wide_count, sub_count, prim)),
        in_specs=[smem, vmem, vmem, vmem, vmem, pl.BlockSpec(memory_space=pl.ANY)],
        out_specs=[vmem, vmem],
        out_shape=[
            jax.ShapeDtypeStruct(residual.shape, F32),
            jax.ShapeDtypeStruct((1, 128), F32),
        ],
        scratch_shapes=[
            pltpu.VMEM(basis_sub.shape, BF16),
            pltpu.VMEM((n, 1, 256), F32),
            pltpu.VMEM((n, 1, 256), F32),
            pltpu.VMEM((ITERS, n, 1, 128), F32),
            pltpu.VMEM((ITERS, n, 1, 128), F32),
            pltpu.VMEM((ITERS + 1, n, 1, 128), F32),
            pltpu.VMEM((ITERS + 1, 1, 128), F32),
            pltpu.SemaphoreType.DMA((2 * ITERS + 2,)),
            pltpu.SemaphoreType.DMA((2 * ITERS + 2,)),
            pltpu.SemaphoreType.DMA,
        ],
        compiler_params=pltpu.CompilerParams(
            collective_id=0, has_side_effects=True, vmem_limit_bytes=32 << 20
        ),
        name="sweeps",
    )(counts, schur, load, high, low, basis_sub)
    return correction, own.reshape(128)


def solution(mesh):
    return jax.shard_map(
        body,
        mesh=mesh,
        in_specs=(
            P(("col", "wide"), None, None),
            P(("col", "wide")),
            P(("col", "wide"), None, None),
            P(("col", "wide"), None),
            P(("col", "wide"), None),
            P(("col", "wide"), None),
            P(),
            P(("col", "wide")),
        ),
        out_specs=(P(("col", "wide"), None), P(("col", "wide"))),
        check_vma=False,
    )
```

```python
import functools

import jax
import jax.numpy as jnp
from jax import lax
from jax.experimental import pallas as pl
from jax.experimental.pallas import tpu as pltpu
from jax.sharding import PartitionSpec as P

ITERS = 3
damping = 0.7
F32 = jnp.float32
BF16 = jnp.bfloat16
MESH = pl.DeviceIdType.MESH
UNROLL = 8


def split2(value):
    high = value.astype(BF16)
    return high, (value - high.astype(F32)).astype(BF16)


def dot(lhs, rhs, left=1, right=0):
    return lax.dot_general(lhs, rhs, (((left,), (right,)), ((), ())), preferred_element_type=F32)


def iota(shape, axis):
    return lax.broadcasted_iota(jnp.int32, shape, axis)


def hot(row, size):
    return (jnp.broadcast_to(row, (size, row.shape[1])) == iota((size, row.shape[1]), 0)).astype(F32)


def rows_sum(value):
    return jnp.sum(value, axis=0, keepdims=True)


def each(first, last, act):
    if last - first <= UNROLL:
        for k in range(first, last):
            act(k)
    else:
        pl.loop(first, last)(act)


def kernel(
    dims, faces_ref, diss_ref, counts_ref, res_ref, primal_ref, owner_ref, flux_ref, basis_ref,
    corr_ref, sol_ref, flux_buf, basis_buf, info_own, info, row_own, rows, hots, lows,
    dense0, denses, send_sem, recv_sem, flux_sem, basis_sem,
):
    col_count, wide_count, sub_count, face_sub, elem_sub, units, prim, chunk = dims
    n = col_count * wide_count
    my_col, my_wide = lax.axis_index("col"), lax.axis_index("wide")

    def wide_peer(k):
        return (my_col, lax.rem(my_wide + k, wide_count))

    def col_peer(k):
        return (lax.rem(my_col + k, col_count), my_wide)

    faces = sub_count * face_sub
    loads = [
        pltpu.make_async_copy(
            flux_ref.at[pl.ds(i * chunk, chunk)], flux_buf.at[pl.ds(i * chunk, chunk)], flux_sem.at[i]
        )
        for i in range(faces // chunk)
    ]
    fetch = pltpu.make_async_copy(basis_ref, basis_buf, basis_sem)
    fetch.start()
    for copy in loads:
        copy.start()

    barrier = pltpu.get_barrier_semaphore()

    def greet(peer):
        def act(k):
            pl.semaphore_signal(barrier, inc=1, device_id=peer(k), device_id_type=MESH)
        return act

    each(1, wide_count, greet(wide_peer))
    each(1, col_count, greet(col_peer))

    owner = owner_ref[...]
    table = jnp.concatenate(
        [(owner >> 7).astype(F32).astype(BF16), (owner & 127).astype(F32).astype(BF16)], axis=1
    )
    highs_f, lows_f = [], []
    for sub in range(sub_count):
        dof = primal_ref[sub:sub + 1, :]
        found = dot(table, hot(dof >> 7, owner.shape[0]).astype(BF16), 0, 0)
        lane = hot(dof & 127, 128)
        highs_f.append(rows_sum(found[:128] * lane))
        lows_f.append(rows_sum(found[128:] * lane))

    fetch.wait()
    schurs, load_rows, diag_rows, alive_rows = [], [], [], []
    for sub in range(sub_count):
        alive_col = (iota((prim, prim), 0) < counts_ref[sub]).astype(F32)
        alive_row = (iota((prim, prim), 1) < counts_ref[sub]).astype(F32)
        schur = jnp.zeros((prim, prim), F32)
        for k in range(face_sub):
            face = sub * face_sub + k
            if face % chunk == 0:
                loads[face // chunk].wait()
            basis_first = basis_buf[sub * elem_sub + faces_ref[0, face]]
            basis_a = basis_first.astype(F32)
            basis_b = basis_buf[sub * elem_sub + faces_ref[1, face]].astype(F32)
            flux = dot(flux_buf[face], (basis_a + basis_b).astype(BF16))
            image = 0.5 * flux + (0.5 * diss_ref[face]) * (basis_a - basis_b)
            schur = schur + dot(basis_first, image.astype(BF16), 0, 0)
        schur = schur * alive_col * alive_row
        flat = basis_buf[sub * elem_sub:(sub + 1) * elem_sub].reshape(elem_sub * units, prim)
        load_rows.append(dot(res_ref[sub:sub + 1, :], flat) * alive_row[:1])
        diag_rows.append(
            rows_sum(schur * (iota((prim, prim), 0) == iota((prim, prim), 1)).astype(F32))
        )
        alive_rows.append(alive_row[:1])
        high, low = split2(schur)
        schurs.append(jnp.concatenate([high, high, low], axis=1))

    info_own[...] = jnp.concatenate(
        [jnp.concatenate(part, axis=1) for part in (load_rows, diag_rows, highs_f, lows_f)], axis=0
    )
    pl.semaphore_wait(barrier, wide_count + col_count - 2)

    def send(source, target, peer, index, count, hop):
        def act(k):
            pltpu.make_async_remote_copy(
                src_ref=source, dst_ref=target.at[index],
                send_sem=send_sem.at[hop], recv_sem=recv_sem.at[hop],
                device_id=peer(k), device_id_type=MESH,
            ).start()

        each(1, count, act)

    def wait(target, count, sem):
        some = target.at[pl.ds(0, count - 1)]
        pltpu.make_async_copy(some, some, sem).wait()

    def to_dense(value_of, parts):
        def add(w, total):
            pieces = [
                piece
                for value in value_of(w)
                for piece in split2(jnp.broadcast_to(value, (n, value.shape[1])) * hots[w].astype(F32))
            ]
            return total + dot(jnp.concatenate(pieces, axis=0), lows[w], 1, 1)

        total = jnp.zeros((2 * parts * n, 128), F32)
        if wide_count <= UNROLL:
            for w in range(wide_count):
                total = add(w, total)
        else:
            total = lax.fori_loop(0, wide_count, add, total)
        return jnp.concatenate(
            [total[2 * i * n:(2 * i + 1) * n] + total[(2 * i + 1) * n:(2 * i + 2) * n] for i in range(parts)],
            axis=0,
        )

    def col_sum(value, target, hop):
        target[my_col] = value
        send(target.at[my_col], target, col_peer, my_col, col_count, hop)
        wait(target, col_count, recv_sem.at[hop])
        total = target[0]
        for c in range(1, col_count):
            total = total + target[c]
        return total

    info[my_wide] = info_own[...]
    send(info_own, info, wide_peer, my_wide, wide_count, 0)
    wait(info, wide_count, recv_sem.at[0])

    def prepare(w):
        hots[w] = hot(info[w, 2:3, :].astype(jnp.int32), n).astype(BF16)
        lows[w] = hot(info[w, 3:4, :].astype(jnp.int32), 128).astype(BF16)

    each(0, wide_count, prepare)
    total = col_sum(
        to_dense(lambda w: [info[w, 0:1, :], info[w, 1:2, :]], 2), dense0, 1
    )
    load = total[:n]
    scale = damping / jnp.maximum(total[n:], 1.0)
    current = load * scale
    my_hot = hot(jnp.concatenate(highs_f, axis=1).astype(jnp.int32), n).astype(BF16)
    my_hot = jnp.concatenate([my_hot, my_hot], axis=0)
    my_low = hot(jnp.concatenate(lows_f, axis=1).astype(jnp.int32), 128)

    def gather(vector):
        return rows_sum(dot(jnp.concatenate(split2(vector), axis=0), my_hot, 0, 0) * my_low)

    for rnd in range(ITERS):
        high, low = split2(gather(current))
        prods = []
        for sub in range(sub_count):
            part = slice(sub * prim, (sub + 1) * prim)
            values = jnp.concatenate([high[:, part], low[:, part], high[:, part]], axis=1)
            prods.append(dot(values, schurs[sub], 1, 1))
        row_own[rnd] = jnp.concatenate(prods, axis=1)
        rows[rnd, my_wide] = row_own[rnd]
        send(row_own.at[rnd], rows.at[rnd], wide_peer, my_wide, wide_count, 2 * rnd + 2)
        wait(rows.at[rnd], wide_count, recv_sem.at[2 * rnd + 2])
        total = col_sum(to_dense(lambda w: [rows[rnd, w]], 1), denses.at[rnd], 2 * rnd + 3)
        current = current + (load - total) * scale

    sol_ref[...] = rows_sum(
        jnp.where(iota((n, 128), 0) == my_col * wide_count + my_wide, current, 0.0)
    )
    near = gather(current)
    for sub in range(sub_count):
        near_sub = (near[:, sub * prim:(sub + 1) * prim] * alive_rows[sub]).astype(BF16)
        flat = basis_buf[sub * elem_sub:(sub + 1) * elem_sub].reshape(elem_sub * units, prim)
        corr_ref[sub:sub + 1, :] = dot(near_sub, flat, 1, 1)

    wait(info, wide_count, send_sem.at[0])
    wait(dense0, col_count, send_sem.at[1])
    for rnd in range(ITERS):
        wait(rows.at[rnd], wide_count, send_sem.at[2 * rnd + 2])
        wait(denses.at[rnd], col_count, send_sem.at[2 * rnd + 3])


def body(flux_jac, dissipation, basis, residual, face_elems, primal, coarse_owner, counts):
    col_count = lax.axis_size("col")
    wide_count = lax.axis_size("wide")
    n = col_count * wide_count
    sub_count = residual.shape[0]
    face_count = flux_jac.shape[0]
    elem_sub = basis.shape[0] // sub_count
    units, prim = basis.shape[1:]
    row_count = sub_count * prim
    chunk = 4
    smem = pl.BlockSpec(memory_space=pltpu.SMEM)
    vmem = pl.BlockSpec(memory_space=pltpu.VMEM)
    hbm = pl.BlockSpec(memory_space=pltpu.HBM)
    hops = 2 * ITERS + 2
    correction, own = pl.pallas_call(
        functools.partial(
            kernel,
            (col_count, wide_count, sub_count, face_count // sub_count, elem_sub, units, prim, chunk),
        ),
        in_specs=[smem, smem, smem, vmem, vmem, vmem, hbm, hbm],
        out_specs=[vmem, vmem],
        out_shape=[
            jax.ShapeDtypeStruct(residual.shape, F32),
            jax.ShapeDtypeStruct((1, 128), F32),
        ],
        scratch_shapes=[
            pltpu.VMEM(flux_jac.shape, BF16),
            pltpu.VMEM(basis.shape, BF16),
            pltpu.VMEM((4, row_count), F32),
            pltpu.VMEM((wide_count, 4, row_count), F32),
            pltpu.VMEM((ITERS, 1, row_count), F32),
            pltpu.VMEM((ITERS, wide_count, 1, row_count), F32),
            pltpu.VMEM((wide_count, n, row_count), BF16),
            pltpu.VMEM((wide_count, 128, row_count), BF16),
            pltpu.VMEM((col_count, 2 * n, 128), F32),
            pltpu.VMEM((ITERS, col_count, n, 128), F32),
            pltpu.SemaphoreType.DMA((hops,)),
            pltpu.SemaphoreType.DMA((hops,)),
            pltpu.SemaphoreType.DMA((face_count // chunk,)),
            pltpu.SemaphoreType.DMA,
        ],
        compiler_params=pltpu.CompilerParams(
            collective_id=0, has_side_effects=True, vmem_limit_bytes=48 << 20
        ),
        name="coarse",
    )(face_elems.T, dissipation, counts, residual, primal, coarse_owner.reshape(-1, 128), flux_jac, basis)
    return correction, own.reshape(128)


def solution(mesh):
    return jax.shard_map(
        body,
        mesh=mesh,
        in_specs=(
            P(("col", "wide"), None, None),
            P(("col", "wide")),
            P(("col", "wide"), None, None),
            P(("col", "wide"), None),
            P(("col", "wide"), None),
            P(("col", "wide"), None),
            P(),
            P(("col", "wide")),
        ),
        out_specs=(P(("col", "wide"), None), P(("col", "wide"))),
        check_vma=False,
    )
```

```python
import functools

import jax
import jax.numpy as jnp
from jax import lax
from jax.experimental import pallas as pl
from jax.experimental.pallas import tpu as pltpu
from jax.sharding import PartitionSpec as P

ITERS = 3
damping = 0.7
F32 = jnp.float32
BF16 = jnp.bfloat16
MESH = pl.DeviceIdType.MESH
UNROLL = 16


def split2(value):
    high = value.astype(BF16)
    return high, (value - high.astype(F32)).astype(BF16)


def dot(lhs, rhs, left=1, right=0):
    return lax.dot_general(lhs, rhs, (((left,), (right,)), ((), ())), preferred_element_type=F32)


def iota(shape, axis):
    return lax.broadcasted_iota(jnp.int32, shape, axis)


def hot(row, size):
    return (jnp.broadcast_to(row, (size, row.shape[1])) == iota((size, row.shape[1]), 0)).astype(F32)


def rows_sum(value):
    return jnp.sum(value, axis=0, keepdims=True)


def each(first, last, act):
    if last - first <= UNROLL:
        for k in range(first, last):
            act(k)
    else:
        pl.loop(first, last)(act)


def kernel(
    dims, faces_ref, diss_ref, counts_ref, res_ref, primal_ref, owner_ref, flux_ref, basis_ref,
    corr_ref, sol_ref, flux_buf, basis_buf, info_own, info, row_own, rows, hots, lows,
    dense0, denses, send_sem, recv_sem, flux_sem, basis_sem,
):
    col_count, wide_count, sub_count, face_sub, elem_sub, units, prim, chunk = dims
    n = col_count * wide_count
    my_col, my_wide = lax.axis_index("col"), lax.axis_index("wide")
    half = wide_count // 2
    groups = col_count * half
    core = lax.rem(my_wide, 2)
    my_group = my_col * half + my_wide // 2

    def group_peer(k):
        to = lax.rem(my_group + groups - k, groups)
        return (to // half, lax.rem(to, half) * 2 + core)

    def core_peer(k):
        return (my_col, my_wide + 1 - 2 * core)

    faces = sub_count * face_sub
    loads = [
        pltpu.make_async_copy(
            flux_ref.at[pl.ds(i * chunk, chunk)], flux_buf.at[pl.ds(i * chunk, chunk)], flux_sem.at[i]
        )
        for i in range(faces // chunk)
    ]
    fetch = pltpu.make_async_copy(basis_ref, basis_buf, basis_sem)
    fetch.start()
    for copy in loads:
        copy.start()

    barrier = pltpu.get_barrier_semaphore()

    def greet(peer):
        def act(k):
            pl.semaphore_signal(barrier, inc=1, device_id=peer(k), device_id_type=MESH)
        return act

    each(1, groups, greet(group_peer))
    each(1, 2, greet(core_peer))

    owner = owner_ref[...]
    table = jnp.concatenate(
        [(owner >> 7).astype(F32).astype(BF16), (owner & 127).astype(F32).astype(BF16)], axis=1
    )
    highs_f, lows_f = [], []
    for sub in range(sub_count):
        dof = primal_ref[sub:sub + 1, :]
        found = dot(table, hot(dof >> 7, owner.shape[0]).astype(BF16), 0, 0)
        lane = hot(dof & 127, 128)
        highs_f.append(rows_sum(found[:128] * lane))
        lows_f.append(rows_sum(found[128:] * lane))

    fetch.wait()
    schurs, load_rows, diag_rows, alive_rows = [], [], [], []
    for sub in range(sub_count):
        alive_col = (iota((prim, prim), 0) < counts_ref[sub]).astype(F32)
        alive_row = (iota((prim, prim), 1) < counts_ref[sub]).astype(F32)
        schur = jnp.zeros((prim, 2 * prim), F32)
        for k in range(face_sub):
            face = sub * face_sub + k
            if face % chunk == 0:
                loads[face // chunk].wait()
            basis_first = basis_buf[sub * elem_sub + faces_ref[0, face]]
            basis_a = basis_first.astype(F32)
            basis_b = basis_buf[sub * elem_sub + faces_ref[1, face]].astype(F32)
            flux = dot(flux_buf[face], (basis_a + basis_b).astype(BF16))
            image = 0.5 * flux + (0.5 * diss_ref[face]) * (basis_a - basis_b)
            schur = schur + dot(basis_first, jnp.concatenate(split2(image), axis=1), 0, 0)
        schur = (schur[:, :prim] + schur[:, prim:]) * alive_col * alive_row
        flat = basis_buf[sub * elem_sub:(sub + 1) * elem_sub].reshape(elem_sub * units, prim)
        load_rows.append(dot(res_ref[sub:sub + 1, :], flat) * alive_row[:1])
        diag_rows.append(
            rows_sum(schur * (iota((prim, prim), 0) == iota((prim, prim), 1)).astype(F32))
        )
        alive_rows.append(alive_row[:1])
        high, low = split2(schur)
        schurs.append(jnp.concatenate([high, high, low], axis=1))

    info_own[...] = jnp.concatenate(
        [jnp.concatenate(part, axis=1) for part in (load_rows, diag_rows, highs_f, lows_f)], axis=0
    )
    pl.semaphore_wait(barrier, groups)

    def send(source, target, peer, index, count, hop):
        def act(k):
            pltpu.make_async_remote_copy(
                src_ref=source, dst_ref=target.at[index],
                send_sem=send_sem.at[hop], recv_sem=recv_sem.at[hop],
                device_id=peer(k), device_id_type=MESH,
            ).start()

        each(1, count, act)

    def wait(target, count, sem):
        some = target.at[pl.ds(0, count - 1)]
        pltpu.make_async_copy(some, some, sem).wait()

    def to_dense(value_of, parts):
        def add(w, total):
            pieces = [
                piece
                for value in value_of(w)
                for piece in split2(jnp.broadcast_to(value, (n, value.shape[1])) * hots[w].astype(F32))
            ]
            return total + dot(jnp.concatenate(pieces, axis=0), lows[w], 1, 1)

        total = jnp.zeros((2 * parts * n, 128), F32)
        if groups <= UNROLL:
            for w in range(groups):
                total = add(w, total)
        else:
            total = lax.fori_loop(0, groups, add, total)
        return jnp.concatenate(
            [total[2 * i * n:(2 * i + 1) * n] + total[(2 * i + 1) * n:(2 * i + 2) * n] for i in range(parts)],
            axis=0,
        )

    def core_sum(value, target, hop):
        target[core] = value
        send(target.at[core], target, core_peer, core, 2, hop)
        wait(target, 2, recv_sem.at[hop])
        return target[0] + target[1]

    info[my_group] = info_own[...]
    send(info_own, info, group_peer, my_group, groups, 0)
    wait(info, groups, recv_sem.at[0])

    def prepare(w):
        hots[w] = hot(info[w, 2:3, :].astype(jnp.int32), n).astype(BF16)
        lows[w] = hot(info[w, 3:4, :].astype(jnp.int32), 128).astype(BF16)

    each(0, groups, prepare)
    total = core_sum(
        to_dense(lambda w: [info[w, 0:1, :], info[w, 1:2, :]], 2), dense0, 1
    )
    load = total[:n]
    scale = damping / jnp.maximum(total[n:], 1.0)
    current = load * scale
    my_hot = hot(jnp.concatenate(highs_f, axis=1).astype(jnp.int32), n).astype(BF16)
    my_hot = jnp.concatenate([my_hot, my_hot], axis=0)
    my_low = hot(jnp.concatenate(lows_f, axis=1).astype(jnp.int32), 128)

    def gather(vector):
        return rows_sum(dot(jnp.concatenate(split2(vector), axis=0), my_hot, 0, 0) * my_low)

    for rnd in range(ITERS):
        high, low = split2(gather(current))
        prods = []
        for sub in range(sub_count):
            part = slice(sub * prim, (sub + 1) * prim)
            values = jnp.concatenate([high[:, part], low[:, part], high[:, part]], axis=1)
            prods.append(dot(values, schurs[sub], 1, 1))
        row_own[rnd] = jnp.concatenate(prods, axis=1)
        rows[rnd, my_group] = row_own[rnd]
        send(row_own.at[rnd], rows.at[rnd], group_peer, my_group, groups, 2 * rnd + 2)
        wait(rows.at[rnd], groups, recv_sem.at[2 * rnd + 2])
        total = core_sum(to_dense(lambda w: [rows[rnd, w]], 1), denses.at[rnd], 2 * rnd + 3)
        current = current + (load - total) * scale

    sol_ref[...] = rows_sum(
        jnp.where(iota((n, 128), 0) == my_col * wide_count + my_wide, current, 0.0)
    )
    near = gather(current)
    for sub in range(sub_count):
        near_sub = (near[:, sub * prim:(sub + 1) * prim] * alive_rows[sub]).astype(BF16)
        flat = basis_buf[sub * elem_sub:(sub + 1) * elem_sub].reshape(elem_sub * units, prim)
        corr_ref[sub:sub + 1, :] = dot(near_sub, flat, 1, 1)

    wait(info, groups, send_sem.at[0])
    wait(dense0, 2, send_sem.at[1])
    for rnd in range(ITERS):
        wait(rows.at[rnd], groups, send_sem.at[2 * rnd + 2])
        wait(denses.at[rnd], 2, send_sem.at[2 * rnd + 3])


def body(flux_jac, dissipation, basis, residual, face_elems, primal, coarse_owner, counts):
    col_count = lax.axis_size("col")
    wide_count = lax.axis_size("wide")
    n = col_count * wide_count
    sub_count = residual.shape[0]
    face_count = flux_jac.shape[0]
    elem_sub = basis.shape[0] // sub_count
    units, prim = basis.shape[1:]
    row_count = sub_count * prim
    chunk = 4
    smem = pl.BlockSpec(memory_space=pltpu.SMEM)
    vmem = pl.BlockSpec(memory_space=pltpu.VMEM)
    hbm = pl.BlockSpec(memory_space=pltpu.HBM)
    hops = 2 * ITERS + 2
    groups = n // 2
    correction, own = pl.pallas_call(
        functools.partial(
            kernel,
            (col_count, wide_count, sub_count, face_count // sub_count, elem_sub, units, prim, chunk),
        ),
        in_specs=[smem, smem, smem, vmem, vmem, vmem, hbm, hbm],
        out_specs=[vmem, vmem],
        out_shape=[
            jax.ShapeDtypeStruct(residual.shape, F32),
            jax.ShapeDtypeStruct((1, 128), F32),
        ],
        scratch_shapes=[
            pltpu.VMEM(flux_jac.shape, BF16),
            pltpu.VMEM(basis.shape, BF16),
            pltpu.VMEM((4, row_count), F32),
            pltpu.VMEM((groups, 4, row_count), F32),
            pltpu.VMEM((ITERS, 1, row_count), F32),
            pltpu.VMEM((ITERS, groups, 1, row_count), F32),
            pltpu.VMEM((groups, n, row_count), BF16),
            pltpu.VMEM((groups, 128, row_count), BF16),
            pltpu.VMEM((2, 2 * n, 128), F32),
            pltpu.VMEM((ITERS, 2, n, 128), F32),
            pltpu.SemaphoreType.DMA((hops,)),
            pltpu.SemaphoreType.DMA((hops,)),
            pltpu.SemaphoreType.DMA((face_count // chunk,)),
            pltpu.SemaphoreType.DMA,
        ],
        compiler_params=pltpu.CompilerParams(
            collective_id=0, has_side_effects=True, vmem_limit_bytes=60 << 20
        ),
        name="coarse",
    )(face_elems.T, dissipation, counts, residual, primal, coarse_owner.reshape(-1, 128), flux_jac, basis)
    return correction, own.reshape(128)


def solution(mesh):
    return jax.shard_map(
        body,
        mesh=mesh,
        in_specs=(
            P(("col", "wide"), None, None),
            P(("col", "wide")),
            P(("col", "wide"), None, None),
            P(("col", "wide"), None),
            P(("col", "wide"), None),
            P(("col", "wide"), None),
            P(),
            P(("col", "wide")),
        ),
        out_specs=(P(("col", "wide"), None), P(("col", "wide"))),
        check_vma=False,
    )
```

```python
import functools

import jax
import jax.numpy as jnp
from jax import lax
from jax.experimental import pallas as pl
from jax.experimental.pallas import tpu as pltpu
from jax.sharding import PartitionSpec as P

ITERS = 3
damping = 0.7
F32 = jnp.float32
BF16 = jnp.bfloat16
MESH = pl.DeviceIdType.MESH
UNROLL = 16


def split2(value):
    high = value.astype(BF16)
    return high, (value - high.astype(F32)).astype(BF16)


def dot(lhs, rhs, left=1, right=0):
    return lax.dot_general(lhs, rhs, (((left,), (right,)), ((), ())), preferred_element_type=F32)


def iota(shape, axis):
    return lax.broadcasted_iota(jnp.int32, shape, axis)


def hot(row, size):
    return (jnp.broadcast_to(row, (size, row.shape[1])) == iota((size, row.shape[1]), 0)).astype(F32)


def rows_sum(value):
    return jnp.sum(value, axis=0, keepdims=True)


def each(first, last, act):
    if last - first <= UNROLL:
        for k in range(first, last):
            act(k)
    else:
        pl.loop(first, last)(act)


def kernel(
    dims, faces_ref, diss_ref, counts_ref, res_ref, primal_ref, owner_ref, flux_ref, basis_ref,
    corr_ref, sol_ref, flux_buf, basis_buf, info_own, info, row_own, rows, hots, lows,
    dense0, denses, send_sem, recv_sem, flux_sem, basis_sem,
):
    col_count, wide_count, sub_count, face_sub, elem_sub, units, prim, chunk = dims
    n = col_count * wide_count
    my_col, my_wide = lax.axis_index("col"), lax.axis_index("wide")
    half = wide_count // 2
    groups = col_count * half
    core = lax.rem(my_wide, 2)
    my_group = my_col * half + my_wide // 2

    def group_peer(k):
        to = lax.rem(my_group + groups - k, groups)
        return (to // half, lax.rem(to, half) * 2 + core)

    def core_peer(k):
        return (my_col, my_wide + 1 - 2 * core)

    faces = sub_count * face_sub
    loads = [
        pltpu.make_async_copy(
            flux_ref.at[pl.ds(i * chunk, chunk)], flux_buf.at[pl.ds(i * chunk, chunk)], flux_sem.at[i]
        )
        for i in range(faces // chunk)
    ]
    fetch = pltpu.make_async_copy(basis_ref, basis_buf, basis_sem)
    fetch.start()
    for copy in loads:
        copy.start()

    barrier = pltpu.get_barrier_semaphore()

    def greet(peer):
        def act(k):
            pl.semaphore_signal(barrier, inc=1, device_id=peer(k), device_id_type=MESH)
        return act

    each(1, groups, greet(group_peer))
    each(1, 2, greet(core_peer))

    owner = owner_ref[...]
    table = jnp.concatenate(
        [(owner >> 7).astype(F32).astype(BF16), (owner & 127).astype(F32).astype(BF16)], axis=1
    )
    highs_f, lows_f = [], []
    for sub in range(sub_count):
        dof = primal_ref[sub:sub + 1, :]
        found = dot(table, hot(dof >> 7, owner.shape[0]).astype(BF16), 0, 0)
        lane = hot(dof & 127, 128)
        highs_f.append(rows_sum(found[:128] * lane))
        lows_f.append(rows_sum(found[128:] * lane))

    fetch.wait()
    schurs, load_rows, diag_rows, alive_rows = [], [], [], []
    for sub in range(sub_count):
        alive_col = (iota((prim, prim), 0) < counts_ref[sub]).astype(F32)
        alive_row = (iota((prim, prim), 1) < counts_ref[sub]).astype(F32)
        schur = jnp.zeros((prim, 2 * prim), F32)
        for k in range(face_sub):
            face = sub * face_sub + k
            if face % chunk == 0:
                loads[face // chunk].wait()
            basis_first = basis_buf[sub * elem_sub + faces_ref[0, face]]
            basis_a = basis_first.astype(F32)
            basis_b = basis_buf[sub * elem_sub + faces_ref[1, face]].astype(F32)
            flux = dot(flux_buf[face], (basis_a + basis_b).astype(BF16))
            image = 0.5 * flux + (0.5 * diss_ref[face]) * (basis_a - basis_b)
            schur = schur + dot(basis_first, jnp.concatenate(split2(image), axis=1), 0, 0)
        schur = (schur[:, :prim] + schur[:, prim:]) * alive_col * alive_row
        flat = basis_buf[sub * elem_sub:(sub + 1) * elem_sub].reshape(elem_sub * units, prim)
        load_rows.append(dot(res_ref[sub:sub + 1, :], flat) * alive_row[:1])
        diag_rows.append(
            rows_sum(schur * (iota((prim, prim), 0) == iota((prim, prim), 1)).astype(F32))
        )
        alive_rows.append(alive_row[:1])
        high, low = split2(schur)
        schurs.append(jnp.concatenate([high, high, low], axis=1))

    info_own[...] = jnp.concatenate(
        [jnp.concatenate(part, axis=1) for part in (load_rows, diag_rows, highs_f, lows_f)], axis=0
    )
    pl.semaphore_wait(barrier, groups)

    def send(source, target, peer, index, count, hop):
        def act(k):
            pltpu.make_async_remote_copy(
                src_ref=source, dst_ref=target.at[index],
                send_sem=send_sem.at[hop], recv_sem=recv_sem.at[hop],
                device_id=peer(k), device_id_type=MESH,
            ).start()

        each(1, count, act)

    def wait(target, count, sem):
        some = target.at[pl.ds(0, count - 1)]
        pltpu.make_async_copy(some, some, sem).wait()

    def to_dense(value_of, parts):
        def add(w, total):
            pieces = [
                piece
                for value in value_of(w)
                for piece in split2(jnp.broadcast_to(value, (n, value.shape[1])) * hots[w].astype(F32))
            ]
            return total + dot(jnp.concatenate(pieces, axis=0), lows[w], 1, 1)

        total = jnp.zeros((2 * parts * n, 128), F32)
        if groups <= UNROLL:
            for w in range(groups):
                total = add(w, total)
        else:
            total = lax.fori_loop(0, groups, add, total)
        return jnp.concatenate(
            [total[2 * i * n:(2 * i + 1) * n] + total[(2 * i + 1) * n:(2 * i + 2) * n] for i in range(parts)],
            axis=0,
        )

    def core_sum(value, target, hop):
        target[core] = value
        send(target.at[core], target, core_peer, core, 2, hop)
        wait(target, 2, recv_sem.at[hop])
        return target[0] + target[1]

    info[my_group] = info_own[...]
    send(info_own, info, group_peer, my_group, groups, 0)
    wait(info, groups, recv_sem.at[0])

    def prepare(w):
        hots[w] = hot(info[w, 2:3, :].astype(jnp.int32), n).astype(BF16)
        lows[w] = hot(info[w, 3:4, :].astype(jnp.int32), 128).astype(BF16)

    each(0, groups, prepare)
    total = core_sum(
        to_dense(lambda w: [info[w, 0:1, :], info[w, 1:2, :]], 2), dense0, 1
    )
    load = total[:n]
    scale = damping / jnp.maximum(total[n:], 1.0)
    current = load * scale
    my_hot = hot(jnp.concatenate(highs_f, axis=1).astype(jnp.int32), n).astype(BF16)
    my_hot = jnp.concatenate([my_hot, my_hot], axis=0)
    my_low = hot(jnp.concatenate(lows_f, axis=1).astype(jnp.int32), 128)

    def gather(vector):
        return rows_sum(dot(jnp.concatenate(split2(vector), axis=0), my_hot, 0, 0) * my_low)

    for rnd in range(ITERS):
        high, low = split2(gather(current))
        prods = []
        for sub in range(sub_count):
            part = slice(sub * prim, (sub + 1) * prim)
            values = jnp.concatenate([high[:, part], low[:, part], high[:, part]], axis=1)
            prods.append(dot(values, schurs[sub], 1, 1))
        row_own[rnd] = jnp.concatenate(prods, axis=1)
        rows[rnd, my_group] = row_own[rnd]
        send(row_own.at[rnd], rows.at[rnd], group_peer, my_group, groups, 2 * rnd + 2)
        wait(rows.at[rnd], groups, recv_sem.at[2 * rnd + 2])
        total = core_sum(to_dense(lambda w: [rows[rnd, w]], 1), denses.at[rnd], 2 * rnd + 3)
        current = current + (load - total) * scale

    sol_ref[...] = rows_sum(
        jnp.where(iota((n, 128), 0) == my_col * wide_count + my_wide, current, 0.0)
    )
    near = gather(current)
    for sub in range(sub_count):
        near_sub = (near[:, sub * prim:(sub + 1) * prim] * alive_rows[sub]).astype(BF16)
        flat = basis_buf[sub * elem_sub:(sub + 1) * elem_sub].reshape(elem_sub * units, prim)
        corr_ref[sub:sub + 1, :] = dot(near_sub, flat, 1, 1)

    wait(info, groups, send_sem.at[0])
    wait(dense0, 2, send_sem.at[1])
    for rnd in range(ITERS):
        wait(rows.at[rnd], groups, send_sem.at[2 * rnd + 2])
        wait(denses.at[rnd], 2, send_sem.at[2 * rnd + 3])


def body(flux_jac, dissipation, basis, residual, face_elems, primal, coarse_owner, counts):
    col_count = lax.axis_size("col")
    wide_count = lax.axis_size("wide")
    n = col_count * wide_count
    sub_count = residual.shape[0]
    face_count = flux_jac.shape[0]
    elem_sub = basis.shape[0] // sub_count
    units, prim = basis.shape[1:]
    row_count = sub_count * prim
    chunk = face_count // sub_count
    smem = pl.BlockSpec(memory_space=pltpu.SMEM)
    vmem = pl.BlockSpec(memory_space=pltpu.VMEM)
    hbm = pl.BlockSpec(memory_space=pltpu.HBM)
    hops = 2 * ITERS + 2
    groups = n // 2
    correction, own = pl.pallas_call(
        functools.partial(
            kernel,
            (col_count, wide_count, sub_count, face_count // sub_count, elem_sub, units, prim, chunk),
        ),
        in_specs=[smem, smem, smem, vmem, vmem, vmem, hbm, hbm],
        out_specs=[vmem, vmem],
        out_shape=[
            jax.ShapeDtypeStruct(residual.shape, F32),
            jax.ShapeDtypeStruct((1, 128), F32),
        ],
        scratch_shapes=[
            pltpu.VMEM(flux_jac.shape, BF16),
            pltpu.VMEM(basis.shape, BF16),
            pltpu.VMEM((4, row_count), F32),
            pltpu.VMEM((groups, 4, row_count), F32),
            pltpu.VMEM((ITERS, 1, row_count), F32),
            pltpu.VMEM((ITERS, groups, 1, row_count), F32),
            pltpu.VMEM((groups, n, row_count), BF16),
            pltpu.VMEM((groups, 128, row_count), BF16),
            pltpu.VMEM((2, 2 * n, 128), F32),
            pltpu.VMEM((ITERS, 2, n, 128), F32),
            pltpu.SemaphoreType.DMA((hops,)),
            pltpu.SemaphoreType.DMA((hops,)),
            pltpu.SemaphoreType.DMA((face_count // chunk,)),
            pltpu.SemaphoreType.DMA,
        ],
        compiler_params=pltpu.CompilerParams(
            collective_id=0, has_side_effects=True, vmem_limit_bytes=60 << 20
        ),
        name="coarse",
    )(face_elems.T, dissipation, counts, residual, primal, coarse_owner.reshape(-1, 128), flux_jac, basis)
    return correction, own.reshape(128)


def solution(mesh):
    return jax.shard_map(
        body,
        mesh=mesh,
        in_specs=(
            P(("col", "wide"), None, None),
            P(("col", "wide")),
            P(("col", "wide"), None, None),
            P(("col", "wide"), None),
            P(("col", "wide"), None),
            P(("col", "wide"), None),
            P(),
            P(("col", "wide")),
        ),
        out_specs=(P(("col", "wide"), None), P(("col", "wide"))),
        check_vma=False,
    )
```
